128 devices in a mesh: gx: 32 (over y, z, core), gy: 4 (over x).
Axes of the slice: x: 4, y: 4, z: 4, core: 2. Of those that a mesh axis runs over, the one named last changes fastest.
Arguments:
- velocity: float32 [3, 512, 64, 1024], P(None, 'gx', 'gy'), may hold values from -6 to 6
- cotangent: float32 [3, 512, 64, 1024], P(None, 'gx', 'gy'), may hold values from -6 to 6
- points: float32 [3, 18432], replicated, as said below
- motion: float32 [3, 18432], replicated, may hold values from -6 to 6
- coef: float32 [49152], P(('gx', 'gy')), may hold values from 0.5 to 4
- readers: int32 [96, 16], replicated, may hold values from 0 to 262143, as said below
- owner: int32 [96], replicated, may hold values from 0 to 127, as said below
Outputs:
- velocity_out: float32 [3, 512, 64, 1024], P(None, 'gx', 'gy')
- coef_grad: float32 [49152], P(('gx', 'gy'))
The draws below stay inside these ranges and needn't reach their ends.
Inputs may be any that keep to these rules, and one draw needn't show every extreme that they name: `readers`: each rotor's 16 tiles form a 4 x 4 block of cells in the first two dimensions at one tile along the third, listed row by row, all on one device; no device holds tiles of more than 4 rotors, and some device holds tiles of exactly 4. `owner`: no device owns more than 2 rotors, and some device owns exactly 2. Each rotor's points lie inside its block of cells in the first two coordinates and inside its tile along the third.
All inputs are finite; a program needn't handle non-finite values.
Results may differ from the reference program's by a relative error of at most 0.0003.
Values sent between devices are 32-bit elements; how exact they have to be, the bound alone decides.
No kernel may reach another device: no remote copies, remote signals or barrier semaphores. Data moves between devices by JAX's collectives and lax.ppermute only.
A program may use at most 64 MiB of HBM per device.

```python
import math
import jax
import jax.numpy as jnp
from jax import lax

CX = 16
CY = 16
CZ = 1024
BOX = 4
HOST_MAX = 4
OWN_MAX = 2
ROTORS = 96
POINTS = 192
NX = 512
NY = 64
KT = 8
SLOTS = 256


def spread_hosts(key, how_many, capacity, devices_all):
    full_dev = jax.random.randint(jax.random.fold_in(key, 1), (), 0, devices_all).astype(jnp.int32)
    others = jax.random.permutation(jax.random.fold_in(key, 2), (devices_all - 1) * capacity)[:how_many - capacity]
    others = (others // capacity).astype(jnp.int32)
    others = others + (others >= full_dev).astype(jnp.int32)
    raw_hosts = jnp.concatenate([jnp.full((capacity,), full_dev, jnp.int32), others])
    shuffle = jax.random.permutation(jax.random.fold_in(key, 3), how_many)
    return raw_hosts[shuffle]


def rotor_blocks(key):
    base = jax.random.fold_in(key, 7)
    dev_y = NY // CY
    devices_all = NX // CX * dev_y
    host_dev = spread_hosts(jax.random.fold_in(base, 11), ROTORS, HOST_MAX, devices_all)
    start_i = host_dev // dev_y * CX + jax.random.randint(jax.random.fold_in(base, 12), (ROTORS,), 0, CX - BOX + 1)
    start_j = host_dev % dev_y * CY + jax.random.randint(jax.random.fold_in(base, 13), (ROTORS,), 0, CY - BOX + 1)
    tile_k = jax.random.randint(jax.random.fold_in(base, 14), (ROTORS,), 0, KT)
    return (start_i.astype(jnp.int32), start_j.astype(jnp.int32), tile_k.astype(jnp.int32))


def draw_readers(key, part):
    start_i, start_j, tile_k = rotor_blocks(key)
    offsets = jnp.arange(BOX, dtype=jnp.int32)
    rows_x = start_i[:, None, None] + offsets[None, :, None]
    rows_y = start_j[:, None, None] + offsets[None, None, :]
    tile_ids = (rows_x * NY + rows_y) * KT + tile_k[:, None, None]
    return tile_ids.reshape(ROTORS, BOX * BOX).astype(jnp.int32)


def draw_points(key, part):
    start_i, start_j, tile_k = rotor_blocks(key)
    noise_x = jax.random.uniform(jax.random.fold_in(key, 31), (ROTORS, POINTS), jnp.float32)
    noise_y = jax.random.uniform(jax.random.fold_in(key, 32), (ROTORS, POINTS), jnp.float32)
    noise_z = jax.random.uniform(jax.random.fold_in(key, 33), (ROTORS, POINTS), jnp.float32)
    coord_x = start_i.astype(jnp.float32)[:, None] + noise_x * (BOX - 1.0)
    coord_y = start_j.astype(jnp.float32)[:, None] + noise_y * (BOX - 1.0)
    coord_z = (tile_k * 128).astype(jnp.float32)[:, None] + 4.0 + noise_z * 120.0
    return jnp.stack([coord_x, coord_y, coord_z]).reshape(3, ROTORS * POINTS).astype(jnp.float32)


def draw_owner(key, part):
    devices_all = NX // CX * (NY // CY)
    return spread_hosts(jax.random.fold_in(key, 23), ROTORS, OWN_MAX, devices_all)


def shard_levels(rng, shape, split, least, high):
    def one(position, parts):
        heights = jax.random.uniform(jax.random.fold_in(jax.random.fold_in(rng, 6), position), (parts,), jnp.float32, least / len(split), high / len(split))
        return jnp.repeat(jnp.exp(heights), shape[position] // parts).reshape((-1,) + (1,) * (len(shape) - position - 1))

    loudness = one(*split[0])
    for cut in split[1:]:
        loudness = loudness * one(*cut)
    return loudness


def centred(stream_key, dims, spread, reach, cuts=(), held_as=jnp.bfloat16):
    level = shard_levels(stream_key, dims, cuts, -0.22, 0.18) if cuts else 1.0
    drawn = jax.random.normal(stream_key, dims, jnp.float32) * spread * level
    return jnp.minimum(jnp.maximum(drawn, -reach), reach).astype(held_as)


def setup_inputs(seed: int = 0) -> dict:
    key_list = jax.random.split(jax.random.key(seed), 8)
    return {
        "velocity": centred(key_list[0], (3, NX, NY, CZ), 1.0, 6.0, ((1, 32), (2, 4)), jnp.float32),
        "cotangent": centred(key_list[1], (3, NX, NY, CZ), 1.0, 6.0, ((1, 32), (2, 4)), jnp.float32),
        "points": draw_points(jax.random.fold_in(key_list[7], 71), 0),
        "motion": centred(key_list[3], (3, ROTORS * POINTS), 1.0, 6.0, (), jnp.float32),
        "coef": jnp.clip(jnp.exp(math.log(4.0) - 2.0794415 * jax.random.uniform(key_list[4], (SLOTS * POINTS,), jnp.float32) ** shard_levels(key_list[4], (SLOTS * POINTS,), ((0, 128),), -0.2, 0.2)), 0.5, 4.0),
        "readers": draw_readers(jax.random.fold_in(key_list[7], 71), 0),
        "owner": draw_owner(jax.random.fold_in(key_list[7], 71), 0),
    }


gauss_norm = math.pi ** (-1.5)
time_step = 0.5
viscosity = 0.15

def cell_kernel(tile_ids, positions, full_y, tiles_z):
    tile_i = tile_ids // (full_y * tiles_z)
    tile_j = tile_ids // tiles_z % full_y
    tile_k = tile_ids % tiles_z
    within = jnp.arange(128, dtype=jnp.int32)
    coord_x = tile_i.astype(jnp.float32)[:, :, None, None]
    coord_y = tile_j.astype(jnp.float32)[:, :, None, None]
    coord_z = (tile_k[:, :, None] * 128 + within[None, None, :]).astype(jnp.float32)[:, :, :, None]
    delta_x = coord_x - positions[0][:, None, None, :]
    delta_y = coord_y - positions[1][:, None, None, :]
    delta_z = coord_z - positions[2][:, None, None, :]
    return gauss_norm * jnp.exp(-(delta_x * delta_x + delta_y * delta_y + delta_z * delta_z))

def laplace_term(padded, center):
    total = padded[:, 2:, 1:-1, 1:-1] + padded[:, :-2, 1:-1, 1:-1]
    total = total + padded[:, 1:-1, 2:, 1:-1] + padded[:, 1:-1, :-2, 1:-1]
    total = total + padded[:, 1:-1, 1:-1, 2:] + padded[:, 1:-1, 1:-1, :-2]
    return total - 6.0 * center

def owner_slots(owner, own_max):
    index = jnp.arange(owner.shape[0], dtype=jnp.int32)
    same = owner[:, None] == owner[None, :]
    earlier = index[None, :] < index[:, None]
    rank_owner = lax.optimization_barrier(jnp.sum((same & earlier).astype(jnp.int32), axis=1)).astype(jnp.int32)
    return (owner * own_max + rank_owner, rank_owner)

def reference(velocity, cotangent, points, motion, coef, readers, owner):
    positions = points.reshape(3, ROTORS, POINTS)
    kernel = cell_kernel(readers, positions, NY, KT)
    slot_ids, rank_owner = owner_slots(owner, OWN_MAX)
    coef_rotor = coef.reshape(SLOTS, POINTS)[slot_ids]
    motion_rot = motion.reshape(3, ROTORS, POINTS)
    flat_readers = readers.reshape(-1)

    def sample(field_in):
        gathered = field_in.reshape(3, NX * NY * KT, 128)[:, readers]
        return jnp.einsum('rtcp,krtc->krp', kernel, gathered, precision=lax.Precision.HIGHEST)

    def substep(velocity_now):
        relative = sample(velocity_now) - motion_rot
        speed = jnp.sqrt(lax.optimization_barrier(jnp.sum(relative * relative, axis=0)))
        shape_term = speed[None] * relative
        force = coef_rotor[None] * shape_term
        contrib = jnp.einsum('rtcp,krp->krtc', kernel, force, precision=lax.Precision.HIGHEST)
        forcing = jnp.zeros((3, NX * NY * KT, 128), jnp.float32)
        forcing = forcing.at[:, flat_readers].add(contrib.reshape(3, -1, 128)).reshape(3, NX, NY, CZ)
        padded = jnp.pad(velocity_now, ((0, 0), (1, 1), (1, 1), (1, 1)))
        return (velocity_now + time_step * (viscosity * laplace_term(padded, velocity_now) + forcing), shape_term)
    velocity_mid, unused_term = substep(velocity)
    velocity_out, shape_second = substep(velocity_mid)
    sampled_adjoint = sample(cotangent)
    grad_rows = time_step * lax.optimization_barrier(jnp.sum(sampled_adjoint * shape_second, axis=0))
    coef_grad = jnp.zeros((SLOTS, POINTS), jnp.float32).at[slot_ids].set(grad_rows).reshape(-1)
    return (velocity_out, coef_grad)
```

```python
import functools
import math

import jax
import jax.numpy as jnp
from jax import lax
from jax.experimental import pallas as pl
from jax.experimental.pallas import tpu as pltpu
from jax.sharding import PartitionSpec as P

AXES = ("gx", "gy")
HOST_MAX = 4
BOX = 4
LANES = 256
FIELDS = 8

gauss_norm = math.pi ** (-1.5)
time_step = 0.5
viscosity = 0.15
HIGH = lax.Precision.HIGHEST

VMEM = pl.BlockSpec(memory_space=pltpu.VMEM)
SMEM = pl.BlockSpec(memory_space=pltpu.SMEM)
HBM = pl.BlockSpec(memory_space=pl.ANY)
PARAMS = pltpu.CompilerParams(vmem_limit_bytes=48 * 2**20)


def log2(value):
    bits = value.bit_length() - 1
    assert 1 << bits == value
    return bits


def gaussians(points, first_i, first_j, first_z, valid):
    cell_z = lax.broadcasted_iota(jnp.int32, (128, LANES), 0) + first_z
    delta_z = cell_z.astype(jnp.float32) - points[2:3]
    along_z = jnp.where(valid, gauss_norm * jnp.exp(-(delta_z * delta_z)), 0.0)
    tile = lax.broadcasted_iota(jnp.int32, (BOX * BOX, LANES), 0)
    delta_x = (lax.shift_right_logical(tile, 2) + first_i).astype(jnp.float32) - points[0:1]
    delta_y = ((tile & 3) + first_j).astype(jnp.float32) - points[1:2]
    across = jnp.exp(-(delta_x * delta_x + delta_y * delta_y))
    return along_z, across


def valid_lanes(odd, points_n):
    lane = lax.broadcasted_iota(jnp.int32, (1, LANES), 1)
    first = odd * (LANES - points_n)
    return (lane >= first) & (lane < first + points_n)


def rotor_at(info_ref, h):
    return [info_ref[h * FIELDS + f] for f in range(FIELDS)]


def reduce_tiles(product, across, k):
    rows = product[k * BOX * BOX : (k + 1) * BOX * BOX]
    return jnp.sum(rows * across, axis=0, keepdims=True)


def sample_kernel(
    rotors, cx_n, cy_n, tiles_z, full_y, points_n, n_gy,
    meta_ref, points_ref, motion_ref, velocity_ref, cotangent_ref,
    info_ref, terms_ref,
    seen_ref, point_ref, move_ref, block_ref, cell_ref, sems,
):
    log_t, log_y = log2(tiles_z), log2(full_y)
    log_cx, log_cy = log2(cx_n), log2(cy_n)
    gx, gy = meta_ref[2 * rotors], meta_ref[2 * rotors + 1]

    def clear(d, carry):
        seen_ref[d] = 0
        return carry

    lax.fori_loop(0, seen_ref.shape[0], clear, 0, unroll=16)

    def visit(r, count):
        tile = meta_ref[r]
        i = lax.shift_right_logical(tile, log_t + log_y)
        j = lax.shift_right_logical(tile, log_t) & (full_y - 1)
        mine = (lax.shift_right_logical(i, log_cx) == gx) & (lax.shift_right_logical(j, log_cy) == gy)
        own = meta_ref[rotors + r]
        earlier = seen_ref[own]
        seen_ref[own] = earlier + 1

        @pl.when(mine)
        def _():
            base = count * FIELDS
            info_ref[base] = r
            info_ref[base + 1] = i
            info_ref[base + 2] = j
            info_ref[base + 3] = tile & (tiles_z - 1)
            info_ref[base + 4] = own
            info_ref[base + 5] = earlier

        return count + mine.astype(jnp.int32)

    count = lax.fori_loop(0, rotors, visit, jnp.int32(0), unroll=8)
    info_ref[HOST_MAX * FIELDS] = count

    def copies(h):
        r, i, j, kz, _, _, _, _ = rotor_at(info_ref, h)
        start = lax.shift_right_logical(r, 1) * (2 * points_n) + (r & 1) * 128
        lanes = pl.ds(pl.multiple_of(start, 128), LANES)
        cells = pl.ds(pl.multiple_of(kz * 128, 128), 128)
        planes = pl.ds(i & (cx_n - 1), BOX)
        return [
            pltpu.make_async_copy(points_ref.at[:, lanes], point_ref.at[h], sems.at[h, 0]),
            pltpu.make_async_copy(motion_ref.at[:, lanes], move_ref.at[h], sems.at[h, 1]),
            pltpu.make_async_copy(velocity_ref.at[:, planes, :, cells], block_ref.at[h, 0], sems.at[h, 2]),
            pltpu.make_async_copy(cotangent_ref.at[:, planes, :, cells], block_ref.at[h, 1], sems.at[h, 3]),
        ]

    for h in range(HOST_MAX):

        @pl.when(h < count)
        def _(h=h):
            for copy in copies(h):
                copy.start()

    for h in range(HOST_MAX):

        @pl.when(h < count)
        def _(h=h):
            for copy in copies(h):
                copy.wait()
            r, i, j, kz, _, _, _, _ = rotor_at(info_ref, h)
            points = point_ref[h]
            along_z, across = gaussians(points, i, j, kz * 128, valid_lanes(r & 1, points_n))
            rows = pl.ds(j & (cy_n - 1), BOX)
            for field in range(2):
                for k in range(3):
                    for a in range(BOX):
                        at = ((field * 3 + k) * BOX + a) * BOX
                        cell_ref[at : at + BOX, :] = block_ref[h, field, k, a, rows, :]
            product = jnp.dot(cell_ref[...], along_z, precision=HIGH, preferred_element_type=jnp.float32)
            move = move_ref[h]
            relative = [reduce_tiles(product, across, k) - move[k : k + 1] for k in range(3)]
            speed = jnp.sqrt(sum(v * v for v in relative))
            for k in range(3):
                terms_ref[h, k : k + 1, :] = speed * relative[k]
                terms_ref[h, 3 + k : 4 + k, :] = reduce_tiles(product, across, 3 + k)
                terms_ref[h, 6 + k : 7 + k, :] = points[k : k + 1]
                terms_ref[h, 9 + k : 10 + k, :] = move[k : k + 1]


def spread(along_z, across, force, cells_ref, block_ref, i, j, kz):
    weighted = jnp.concatenate([across * force[k] for k in range(3)], axis=0)
    contrib = lax.dot_general(
        weighted, along_z, (((1,), (1,)), ((), ())), precision=HIGH, preferred_element_type=jnp.float32
    )
    where = (slice(None), pl.ds(i, BOX), slice(None), pl.ds(pl.multiple_of(kz * 128, 128), 128))
    block_ref[...] = cells_ref[where]
    for k in range(3):
        for a in range(BOX):
            at = (k * BOX + a) * BOX
            rows = (k, a, pl.ds(j, BOX))
            block_ref[rows] = block_ref[rows] + time_step * contrib[at : at + BOX]
    cells_ref[where] = block_ref[...]


def force_kernel(
    cx_n, cy_n, points_n,
    info_ref, terms_ref, table_ref, start_ref,
    mid_ref, x_low_ref, x_high_ref, y_low_ref, y_high_ref, send_ref, force_ref,
    cell_ref, block_ref,
):
    count = info_ref[HOST_MAX * FIELDS]
    mid_ref[...] = start_ref[...]
    send_ref[...] = jnp.zeros_like(send_ref)

    def setup(h):
        r, i, j, kz, own, rank, _, _ = rotor_at(info_ref, h)
        points = terms_ref[h, 6:9, :]
        along_z, across = gaussians(points, i, j, kz * 128, valid_lanes(r & 1, points_n))
        here = (i & (cx_n - 1), j & (cy_n - 1), kz)
        row = table_ref[pl.ds(own, 1), :]
        coef = jnp.where(rank > 0, row[:, 128:], row[:, :LANES])
        shifted_up = pltpu.roll(coef, LANES - points_n, 1)
        shifted_down = pltpu.roll(coef, points_n, 1)
        odd = r & 1
        coef = jnp.where(rank == odd, coef, jnp.where(rank < odd, shifted_up, shifted_down))
        return along_z, across, here, coef, odd, own, rank

    for h in range(HOST_MAX):

        @pl.when(h < count)
        def _(h=h):
            along_z, across, here, coef, _, _, _ = setup(h)
            force = [coef * terms_ref[h, k : k + 1, :] for k in range(3)]
            spread(along_z, across, force, mid_ref, block_ref, *here)

    for h in range(HOST_MAX):

        @pl.when(h < count)
        def _(h=h):
            along_z, across, (i, j, kz), coef, odd, own, rank = setup(h)
            cells = pl.ds(pl.multiple_of(kz * 128, 128), 128)
            block_ref[...] = mid_ref[:, pl.ds(i, BOX), :, cells]
            for k in range(3):
                for a in range(BOX):
                    at = (k * BOX + a) * BOX
                    cell_ref[at : at + BOX, :] = block_ref[k, a, pl.ds(j, BOX)]
            product = jnp.dot(cell_ref[...], along_z, precision=HIGH, preferred_element_type=jnp.float32)
            relative = [reduce_tiles(product, across, k) - terms_ref[h, 9 + k : 10 + k, :] for k in range(3)]
            speed = jnp.sqrt(sum(v * v for v in relative))
            grad = jnp.zeros((1, LANES), jnp.float32)
            for k in range(3):
                shape_term = speed * relative[k]
                grad = grad + terms_ref[h, 3 + k : 4 + k, :] * shape_term
                force_ref[h, k : k + 1, :] = coef * shape_term
            for k in range(3):
                force_ref[h, 3 + k : 4 + k, :] = terms_ref[h, 6 + k : 7 + k, :]
            grad = time_step * grad
            shifted_up = pltpu.roll(grad, LANES - points_n, 1)
            shifted_down = pltpu.roll(grad, points_n, 1)
            grad = jnp.where(rank == odd, grad, jnp.where(odd < rank, shifted_up, shifted_down))
            blank = jnp.zeros((1, 128), jnp.float32)
            wide = jnp.where(
                rank > 0, jnp.concatenate([blank, grad], axis=1), jnp.concatenate([grad, blank], axis=1)
            )
            send_ref[pl.ds(own, 1), :] = send_ref[pl.ds(own, 1), :] + wide

    x_low_ref[...] = mid_ref[:, 0]
    x_high_ref[...] = mid_ref[:, cx_n - 1]
    for x in range(cx_n):
        y_low_ref[:, x : x + 1] = mid_ref[:, x, 0:1]
        y_high_ref[:, x : x + 1] = mid_ref[:, x, cy_n - 1 : cy_n]


def substep_kernel(
    cx_n, cy_n, cz_n, points_n, n_gx, n_gy, gx_at, forced,
    *refs,
):
    if forced:
        meta_ref, info_ref, force_ref, now_ref, x_low_ref, x_high_ref, y_low_ref, y_high_ref, next_ref, block_ref = refs
    else:
        meta_ref, now_ref, x_low_ref, x_high_ref, y_low_ref, y_high_ref, next_ref = refs
    gx, gy = meta_ref[gx_at], meta_ref[gx_at + 1]
    row = lax.broadcasted_iota(jnp.int32, (cy_n, cz_n), 0)
    lane = lax.broadcasted_iota(jnp.int32, (cy_n, cz_n), 1)
    rate = time_step * viscosity
    has_x_low = (gx > 0).astype(jnp.float32)
    has_x_high = (gx < n_gx - 1).astype(jnp.float32)
    has_y_low = (gy > 0).astype(jnp.float32)
    has_y_high = (gy < n_gy - 1).astype(jnp.float32)

    def plane(x, below, above, k):
        now = now_ref[k, x]
        y_below = jnp.where(row == 0, y_low_ref[k, pl.ds(x, 1)] * has_y_low, pltpu.roll(now, 1, 0))
        y_above = jnp.where(
            row == cy_n - 1, y_high_ref[k, pl.ds(x, 1)] * has_y_high, pltpu.roll(now, cy_n - 1, 0)
        )
        z_below = jnp.where(lane == 0, 0.0, pltpu.roll(now, 1, 1))
        z_above = jnp.where(lane == cz_n - 1, 0.0, pltpu.roll(now, cz_n - 1, 1))
        total = (below + above) + (y_below + y_above) + (z_below + z_above)
        next_ref[k, x] = now + rate * (total - 6.0 * now)

    for k in range(3):
        plane(0, x_low_ref[k] * has_x_low, now_ref[k, 1], k)
        plane(cx_n - 1, now_ref[k, cx_n - 2], x_high_ref[k] * has_x_high, k)

        def inner(x, carry, k=k):
            plane(x, now_ref[k, x - 1], now_ref[k, x + 1], k)
            return carry

        lax.fori_loop(1, cx_n - 1, inner, 0)

    if forced:
        count = info_ref[HOST_MAX * FIELDS]
        for h in range(HOST_MAX):

            @pl.when(h < count)
            def _(h=h):
                r, i, j, kz, _, _, _, _ = rotor_at(info_ref, h)
                along_z, across = gaussians(
                    force_ref[h, 3:6, :], i, j, kz * 128, valid_lanes(r & 1, points_n)
                )
                force = [force_ref[h, k : k + 1, :] for k in range(3)]
                spread(along_z, across, force, next_ref, block_ref, i & (cx_n - 1), j & (cy_n - 1), kz)


def ring(count, step):
    return [(i, (i + step) % count) for i in range(count)]


def exchange(faces, n_gx, n_gy):
    x_low, x_high, y_low, y_high = faces
    return (
        lax.ppermute(x_high, "gx", ring(n_gx, 1)),
        lax.ppermute(x_low, "gx", ring(n_gx, -1)),
        lax.ppermute(y_high, "gy", ring(n_gy, 1)),
        lax.ppermute(y_low, "gy", ring(n_gy, -1)),
    )


def per_device(velocity, cotangent, points, motion, coef, readers, owner):
    _, cx_n, cy_n, cz_n = velocity.shape
    tiles_z = cz_n // 128
    n_gx, n_gy = lax.axis_size("gx"), lax.axis_size("gy")
    devices = n_gx * n_gy
    full_y = cy_n * n_gy
    rotors = readers.shape[0]
    points_n = points.shape[1] // rotors
    own_n = coef.shape[0]
    f32 = jnp.float32

    meta = jnp.concatenate(
        [readers[:, 0], owner, lax.axis_index("gx")[None], lax.axis_index("gy")[None]]
    ).astype(jnp.int32)
    table = lax.all_to_all(jnp.broadcast_to(coef[None], (devices, own_n)), AXES, 0, 0, tiled=True)
    faces = (velocity[:, 0], velocity[:, cx_n - 1], velocity[:, :, 0], velocity[:, :, cy_n - 1])
    halos = exchange(faces, n_gx, n_gy)

    info, terms = pl.pallas_call(
        functools.partial(sample_kernel, rotors, cx_n, cy_n, tiles_z, full_y, points_n, n_gy),
        out_shape=(
            jax.ShapeDtypeStruct((64,), jnp.int32),
            jax.ShapeDtypeStruct((HOST_MAX, 16, LANES), f32),
        ),
        in_specs=[SMEM, HBM, HBM, HBM, HBM],
        out_specs=(SMEM, VMEM),
        scratch_shapes=[
            pltpu.SMEM((devices,), jnp.int32),
            pltpu.VMEM((HOST_MAX, 3, LANES), f32),
            pltpu.VMEM((HOST_MAX, 3, LANES), f32),
            pltpu.VMEM((HOST_MAX, 2, 3, BOX, cy_n, 128), f32),
            pltpu.VMEM((6 * BOX * BOX, 128), f32),
            pltpu.SemaphoreType.DMA((HOST_MAX, 4)),
        ],
        compiler_params=PARAMS,
        name="sample",
    )(meta, points, motion, velocity, cotangent)

    def substep(now, halos, extra):
        return pl.pallas_call(
            functools.partial(
                substep_kernel, cx_n, cy_n, cz_n, points_n, n_gx, n_gy, 2 * rotors, bool(extra)
            ),
            out_shape=jax.ShapeDtypeStruct(velocity.shape, f32),
            in_specs=[SMEM] + ([SMEM, VMEM] if extra else []) + [VMEM] * 5,
            out_specs=VMEM,
            scratch_shapes=[pltpu.VMEM((3, BOX, cy_n, 128), f32)] if extra else [],
            compiler_params=PARAMS,
            name="substep",
        )(meta, *extra, now, *halos)

    start = substep(velocity, halos, ())
    face_x = jax.ShapeDtypeStruct((3, cy_n, cz_n), f32)
    face_y = jax.ShapeDtypeStruct((3, cx_n, cz_n), f32)
    mid, x_low, x_high, y_low, y_high, send, force = pl.pallas_call(
        functools.partial(force_kernel, cx_n, cy_n, points_n),
        out_shape=(
            jax.ShapeDtypeStruct(velocity.shape, f32), face_x, face_x, face_y, face_y,
            jax.ShapeDtypeStruct((devices, own_n), f32),
            jax.ShapeDtypeStruct((HOST_MAX, 8, LANES), f32),
        ),
        in_specs=[SMEM, VMEM, VMEM, VMEM],
        out_specs=(VMEM,) * 7,
        scratch_shapes=[
            pltpu.VMEM((3 * BOX * BOX, 128), f32),
            pltpu.VMEM((3, BOX, cy_n, 128), f32),
        ],
        compiler_params=PARAMS,
        name="force",
    )(info, terms, table, start)
    received = lax.all_to_all(send, AXES, 0, 0, tiled=True)
    halos = exchange((x_low, x_high, y_low, y_high), n_gx, n_gy)
    velocity_out = substep(mid, halos, (info, force))
    return velocity_out, jnp.sum(received, axis=0)


def solution(mesh):
    cells = P(None, "gx", "gy", None)
    return jax.shard_map(
        per_device,
        mesh=mesh,
        in_specs=(cells, cells, P(), P(), P(AXES), P(), P()),
        out_specs=(cells, P(AXES)),
        check_vma=False,
    )
```

```python
import functools
import math

import jax
import jax.numpy as jnp
from jax import lax
from jax.experimental import pallas as pl
from jax.experimental.pallas import tpu as pltpu
from jax.sharding import PartitionSpec as P

AXES = ("gx", "gy")
HOST_MAX = 4
BOX = 4
LANES = 256
UNROLL = 14
FIELDS = 8

gauss_norm = math.pi ** (-1.5)
time_step = 0.5
viscosity = 0.15
HIGH = lax.Precision.HIGHEST

VMEM = pl.BlockSpec(memory_space=pltpu.VMEM)
SMEM = pl.BlockSpec(memory_space=pltpu.SMEM)
HBM = pl.BlockSpec(memory_space=pltpu.HBM)
PARAMS = pltpu.CompilerParams(vmem_limit_bytes=24 * 2**20)


def log2(value):
    bits = value.bit_length() - 1
    assert 1 << bits == value
    return bits


def gaussians(points, first_i, first_j, first_z, valid):
    cell_z = lax.broadcasted_iota(jnp.int32, (128, LANES), 0) + first_z
    delta_z = cell_z.astype(jnp.float32) - points[2:3]
    along_z = jnp.where(valid, gauss_norm * jnp.exp(-(delta_z * delta_z)), 0.0)
    tile = lax.broadcasted_iota(jnp.int32, (BOX * BOX, LANES), 0)
    delta_x = (lax.shift_right_logical(tile, 2) + first_i).astype(jnp.float32) - points[0:1]
    delta_y = ((tile & 3) + first_j).astype(jnp.float32) - points[1:2]
    across = jnp.exp(-(delta_x * delta_x + delta_y * delta_y))
    return along_z, across


def valid_lanes(odd, points_n):
    lane = lax.broadcasted_iota(jnp.int32, (1, LANES), 1)
    first = odd * (LANES - points_n)
    return (lane >= first) & (lane < first + points_n)


def rotor_at(info_ref, h):
    return [info_ref[h * FIELDS + f] for f in range(FIELDS)]


def reduce_tiles(product, across, k):
    rows = product[k * BOX * BOX : (k + 1) * BOX * BOX]
    return jnp.sum(rows * across, axis=0, keepdims=True)


def sample_kernel(
    rotors, cx_n, cy_n, tiles_z, full_y, points_n, n_gy,
    meta_ref, points_ref, motion_ref, velocity_ref, cotangent_ref,
    info_ref, terms_ref,
    seen_ref, point_ref, move_ref, block_ref, cell_ref, sems,
):
    log_t, log_y = log2(tiles_z), log2(full_y)
    log_cx, log_cy = log2(cx_n), log2(cy_n)
    gx, gy = meta_ref[2 * rotors], meta_ref[2 * rotors + 1]

    def clear(d, carry):
        seen_ref[d] = 0
        return carry

    lax.fori_loop(0, seen_ref.shape[0], clear, 0, unroll=16)

    def visit(r, count):
        tile = meta_ref[r]
        i = lax.shift_right_logical(tile, log_t + log_y)
        j = lax.shift_right_logical(tile, log_t) & (full_y - 1)
        mine = (lax.shift_right_logical(i, log_cx) == gx) & (lax.shift_right_logical(j, log_cy) == gy)
        own = meta_ref[rotors + r]
        earlier = seen_ref[own]
        seen_ref[own] = earlier + 1

        @pl.when(mine)
        def _():
            base = count * FIELDS
            info_ref[base] = r
            info_ref[base + 1] = i
            info_ref[base + 2] = j
            info_ref[base + 3] = tile & (tiles_z - 1)
            info_ref[base + 4] = own
            info_ref[base + 5] = earlier

        return count + mine.astype(jnp.int32)

    count = lax.fori_loop(0, rotors, visit, jnp.int32(0), unroll=8)
    info_ref[HOST_MAX * FIELDS] = count

    def copies(h):
        r, i, _, kz, _, _, _, _ = rotor_at(info_ref, h)
        start = lax.shift_right_logical(r, 1) * (2 * points_n) + (r & 1) * 128
        lanes = pl.ds(pl.multiple_of(start, 128), LANES)
        cells = pl.ds(pl.multiple_of(kz * 128, 128), 128)
        planes = pl.ds(i & (cx_n - 1), BOX)
        return [
            pltpu.make_async_copy(points_ref.at[:, lanes], point_ref.at[h], sems.at[h, 0]),
            pltpu.make_async_copy(motion_ref.at[:, lanes], move_ref.at[h], sems.at[h, 1]),
            pltpu.make_async_copy(velocity_ref.at[:, planes, :, cells], block_ref.at[h, 0], sems.at[h, 2]),
            pltpu.make_async_copy(cotangent_ref.at[:, planes, :, cells], block_ref.at[h, 1], sems.at[h, 3]),
        ]

    for h in range(HOST_MAX):

        @pl.when(h < count)
        def _(h=h):
            for copy in copies(h):
                copy.start()

    for h in range(HOST_MAX):

        @pl.when(h < count)
        def _(h=h):
            for copy in copies(h):
                copy.wait()
            r, i, j, kz, _, _, _, _ = rotor_at(info_ref, h)
            points, move = point_ref[h], move_ref[h]
            along_z, across = gaussians(points, i, j, kz * 128, valid_lanes(r & 1, points_n))
            rows = pl.ds(j & (cy_n - 1), BOX)
            for field in range(2):
                for k in range(3):
                    for a in range(BOX):
                        at = ((field * 3 + k) * BOX + a) * BOX
                        cell_ref[at : at + BOX, :] = block_ref[h, field, k, a, rows, :]
            product = jnp.dot(cell_ref[...], along_z, precision=HIGH, preferred_element_type=jnp.float32)
            relative = [reduce_tiles(product, across, k) - move[k : k + 1] for k in range(3)]
            speed = jnp.sqrt(sum(v * v for v in relative))
            for k in range(3):
                terms_ref[h, k : k + 1, :] = speed * relative[k]
                terms_ref[h, 3 + k : 4 + k, :] = reduce_tiles(product, across, 3 + k)
                terms_ref[h, 6 + k : 7 + k, :] = points[k : k + 1]
                terms_ref[h, 9 + k : 10 + k, :] = move[k : k + 1]


def spread(along_z, across, force, part_ref, h, j):
    weighted = jnp.concatenate([across * force[k] for k in range(3)], axis=0)
    contrib = lax.dot_general(
        weighted, along_z, (((1,), (1,)), ((), ())), precision=HIGH, preferred_element_type=jnp.float32
    )
    part_ref[h] = jnp.zeros(part_ref.shape[1:], jnp.float32)
    for k in range(3):
        for a in range(BOX):
            at = (k * BOX + a) * BOX
            part_ref[h, k, a, pl.ds(j, BOX)] = time_step * contrib[at : at + BOX]


def add_forces(info_ref, count, part_ref, next_ref, k):
    cx_n = next_ref.shape[1]
    for h in range(HOST_MAX):

        @pl.when(h < count)
        def _(h=h):
            _, i, _, kz, _, _, _, _ = rotor_at(info_ref, h)
            cells = pl.ds(pl.multiple_of(kz * 128, 128), 128)
            where = (k, pl.ds(i & (cx_n - 1), BOX), slice(None), cells)
            next_ref[where] = next_ref[where] + part_ref[h, k]


def laplace(meta_ref, gx_at, n_gx, n_gy, now_ref, halo_refs, next_ref, before, after_each):
    x_low_ref, x_high_ref, y_low_ref, y_high_ref = halo_refs
    _, cx_n, cy_n, cz_n = now_ref.shape
    gx, gy = meta_ref[gx_at], meta_ref[gx_at + 1]
    rate = time_step * viscosity
    subs, tiles = cy_n // 8, cz_n // 128
    row = lax.broadcasted_iota(jnp.int32, (8, 128), 0)
    lane = lax.broadcasted_iota(jnp.int32, (8, 128), 1)
    first_row, last_row, first_lane, last_lane = row == 0, row == 7, lane == 0, lane == 127
    zero = jnp.zeros((8, 128), jnp.float32)

    def flag(condition):
        return jnp.where(condition, 1.0, 0.0).astype(jnp.float32)

    has_x_low, has_x_high = flag(gx > 0), flag(gx < n_gx - 1)
    has_y_low, has_y_high = flag(gy > 0), flag(gy < n_gy - 1)

    def plane(k, x, below, above):
        def at(s, j):
            return now_ref[k, x, s * 8 : s * 8 + 8, j * 128 : j * 128 + 128]

        now = [[at(s, j) for j in range(tiles)] for s in range(subs)]
        for j in range(tiles):
            lanes = slice(j * 128, j * 128 + 128)
            up = [pltpu.roll(now[s][j], 1, 0) for s in range(subs)]
            down = [pltpu.roll(now[s][j], 7, 0) for s in range(subs)]
            low = jnp.broadcast_to(y_low_ref[k, x, :, lanes] * has_y_low, (8, 128))
            high = jnp.broadcast_to(y_high_ref[k, x, :, lanes] * has_y_high, (8, 128))
            for s in range(subs):
                here = now[s][j]
                y_below = jnp.where(first_row, up[s - 1] if s else low, up[s])
                y_above = jnp.where(last_row, down[s + 1] if s < subs - 1 else high, down[s])
                before = pltpu.roll(now[s][j - 1], 1, 1) if j else zero
                after = pltpu.roll(now[s][j + 1], 127, 1) if j < tiles - 1 else zero
                z_below = jnp.where(first_lane, before, pltpu.roll(here, 1, 1))
                z_above = jnp.where(last_lane, after, pltpu.roll(here, 127, 1))
                total = (below(s, j) + above(s, j)) + (y_below + y_above) + (z_below + z_above)
                next_ref[k, x, s * 8 : s * 8 + 8, lanes] = (1.0 - 6.0 * rate) * here + rate * total

    def inside(k, x):
        return lambda s, j: now_ref[k, x, s * 8 : s * 8 + 8, j * 128 : j * 128 + 128]

    def outside(ref, k, scale):
        return lambda s, j: ref[k, s * 8 : s * 8 + 8, j * 128 : j * 128 + 128] * scale

    def component(k, carry):
        before(k)
        plane(k, 0, outside(x_low_ref, k, has_x_low), inside(k, 1))
        plane(k, cx_n - 1, inside(k, cx_n - 2), outside(x_high_ref, k, has_x_high))

        def inner(x, carry):
            plane(k, x, inside(k, x - 1), inside(k, x + 1))
            return carry

        lax.fori_loop(1, cx_n - 1, inner, 0, unroll=UNROLL)
        after_each(k)
        return carry

    lax.fori_loop(0, 3, component, 0)


def aligned(value, rank, odd, points_n):
    earlier = pltpu.roll(value, LANES - points_n, 1)
    later = pltpu.roll(value, points_n, 1)
    return jnp.where(rank == odd, value, jnp.where(rank < odd, earlier, later))


def advance_kernel(
    points_n, gx_at, n_gx, n_gy,
    meta_ref, info_ref, terms_ref, table_ref, field_ref, hx_low_ref, hx_high_ref, hy_low_ref, hy_high_ref,
    out_ref, x_low_ref, x_high_ref, y_low_ref, y_high_ref, send_ref, force_ref,
    now_ref, mid_ref, part_ref, cell_ref, block_ref, sems,
):
    _, cx_n, cy_n, _ = now_ref.shape
    count = info_ref[HOST_MAX * FIELDS]

    def load(k):
        return pltpu.make_async_copy(field_ref.at[k], now_ref.at[k], sems.at[k])

    def save(k):
        return pltpu.make_async_copy(mid_ref.at[k], out_ref.at[k], sems.at[3 + k])

    for k in range(3):
        load(k).start()
    send_ref[...] = jnp.zeros_like(send_ref)

    def setup(h):
        r, i, j, kz, own, rank, _, _ = rotor_at(info_ref, h)
        along_z, across = gaussians(terms_ref[h, 6:9, :], i, j, kz * 128, valid_lanes(r & 1, points_n))
        row = table_ref[own]
        coef = jnp.where(rank > 0, row[:, 128:], row[:, :LANES])
        return along_z, across, (i & (cx_n - 1), j & (cy_n - 1), kz), aligned(coef, rank, r & 1, points_n)

    for h in range(HOST_MAX):

        @pl.when(h < count)
        def _(h=h):
            along_z, across, here, coef = setup(h)
            force = [coef * terms_ref[h, k : k + 1, :] for k in range(3)]
            spread(along_z, across, force, part_ref, h, here[1])

    def after(k):
        add_forces(info_ref, count, part_ref, mid_ref, k)
        save(k).start()

    halo_refs = (hx_low_ref, hx_high_ref, hy_low_ref, hy_high_ref)
    laplace(meta_ref, gx_at, n_gx, n_gy, now_ref, halo_refs, mid_ref, lambda k: load(k).wait(), after)

    for h in range(HOST_MAX):

        @pl.when(h < count)
        def _(h=h):
            along_z, across, (i, j, kz), coef = setup(h)
            r, _, _, _, own, rank, _, _ = rotor_at(info_ref, h)
            block_ref[...] = mid_ref[:, pl.ds(i, BOX), :, pl.ds(pl.multiple_of(kz * 128, 128), 128)]
            for k in range(3):
                for a in range(BOX):
                    at = (k * BOX + a) * BOX
                    cell_ref[at : at + BOX, :] = block_ref[k, a, pl.ds(j, BOX)]
            product = jnp.dot(cell_ref[...], along_z, precision=HIGH, preferred_element_type=jnp.float32)
            relative = [reduce_tiles(product, across, k) - terms_ref[h, 9 + k : 10 + k, :] for k in range(3)]
            speed = jnp.sqrt(sum(v * v for v in relative))
            grad = jnp.zeros((1, LANES), jnp.float32)
            for k in range(3):
                shape_term = speed * relative[k]
                grad = grad + terms_ref[h, 3 + k : 4 + k, :] * shape_term
                force_ref[h, k : k + 1, :] = coef * shape_term
            for k in range(3):
                force_ref[h, 3 + k : 4 + k, :] = terms_ref[h, 6 + k : 7 + k, :]
            grad = aligned(time_step * grad, r & 1, rank, points_n)
            blank = jnp.zeros((1, 128), jnp.float32)
            wide = jnp.where(
                rank > 0, jnp.concatenate([blank, grad], axis=1), jnp.concatenate([grad, blank], axis=1)
            )
            send_ref[own] = send_ref[own] + wide

    for k in range(3):
        write_faces(mid_ref, x_low_ref, x_high_ref, y_low_ref, y_high_ref, k)
    for k in range(3):
        save(k).wait()


def write_faces(field_ref, x_low_ref, x_high_ref, y_low_ref, y_high_ref, k):
    _, cx_n, cy_n, _ = field_ref.shape
    x_low_ref[k] = field_ref[k, 0]
    x_high_ref[k] = field_ref[k, cx_n - 1]
    for x in range(cx_n):
        y_low_ref[k, x] = field_ref[k, x, 0:1]
        y_high_ref[k, x] = field_ref[k, x, cy_n - 1 : cy_n]


def faces_kernel(field_ref, x_low_ref, x_high_ref, y_low_ref, y_high_ref, now_ref, sems):
    def load(k):
        return pltpu.make_async_copy(field_ref.at[k], now_ref.at[k], sems.at[k])

    for k in range(3):
        load(k).start()
    for k in range(3):
        load(k).wait()
        write_faces(now_ref, x_low_ref, x_high_ref, y_low_ref, y_high_ref, k)


def finish_kernel(
    points_n, gx_at, n_gx, n_gy,
    meta_ref, info_ref, force_ref, field_ref, x_low_ref, x_high_ref, y_low_ref, y_high_ref,
    out_ref,
    now_ref, next_ref, part_ref, sems,
):
    _, cx_n, cy_n, _ = now_ref.shape

    def load(k):
        return pltpu.make_async_copy(field_ref.at[k], now_ref.at[k], sems.at[k])

    def save(k):
        return pltpu.make_async_copy(next_ref.at[k], out_ref.at[k], sems.at[3 + k])

    for k in range(3):
        load(k).start()
    count = info_ref[HOST_MAX * FIELDS]
    for h in range(HOST_MAX):

        @pl.when(h < count)
        def _(h=h):
            r, i, j, kz, _, _, _, _ = rotor_at(info_ref, h)
            along_z, across = gaussians(force_ref[h, 3:6, :], i, j, kz * 128, valid_lanes(r & 1, points_n))
            force = [force_ref[h, k : k + 1, :] for k in range(3)]
            spread(along_z, across, force, part_ref, h, j & (cy_n - 1))

    def after(k):
        add_forces(info_ref, count, part_ref, next_ref, k)
        save(k).start()

    halo_refs = (x_low_ref, x_high_ref, y_low_ref, y_high_ref)
    laplace(meta_ref, gx_at, n_gx, n_gy, now_ref, halo_refs, next_ref, lambda k: load(k).wait(), after)
    for k in range(3):
        save(k).wait()


def ring(count, step):
    return [(i, (i + step) % count) for i in range(count)]


def exchange(faces, n_gx, n_gy):
    x_low, x_high, y_low, y_high = faces
    return (
        lax.ppermute(x_high, "gx", ring(n_gx, 1)),
        lax.ppermute(x_low, "gx", ring(n_gx, -1)),
        lax.ppermute(y_high, "gy", ring(n_gy, 1)),
        lax.ppermute(y_low, "gy", ring(n_gy, -1)),
    )


def per_device(velocity, cotangent, points, motion, coef, readers, owner):
    velocity, cotangent, points, motion = (
        pltpu.with_memory_space_constraint(array, pltpu.HBM) for array in (velocity, cotangent, points, motion)
    )
    _, cx_n, cy_n, cz_n = velocity.shape
    tiles_z = cz_n // 128
    n_gx, n_gy = lax.axis_size("gx"), lax.axis_size("gy")
    devices = n_gx * n_gy
    full_y = cy_n * n_gy
    rotors = readers.shape[0]
    points_n = points.shape[1] // rotors
    own_n = coef.shape[0]
    f32 = jnp.float32
    field = pltpu.HBM(velocity.shape, f32)
    face_x = jax.ShapeDtypeStruct((3, cy_n, cz_n), f32)
    face_y = jax.ShapeDtypeStruct((3, cx_n, 1, cz_n), f32)
    faces = (face_x, face_x, face_y, face_y)
    rows = jax.ShapeDtypeStruct((devices, 1, own_n), f32)

    table = lax.all_to_all(jnp.broadcast_to(coef[None, None], (devices, 1, own_n)), AXES, 0, 0, tiled=True)
    meta = jnp.concatenate(
        [readers[:, 0], owner, lax.axis_index("gx")[None], lax.axis_index("gy")[None]]
    ).astype(jnp.int32)
    halos = exchange(
        pl.pallas_call(
            faces_kernel, out_shape=faces, in_specs=[HBM], out_specs=(VMEM,) * 4,
            scratch_shapes=[pltpu.VMEM(velocity.shape, f32), pltpu.SemaphoreType.DMA((3,))],
            compiler_params=PARAMS, name="faces",
        )(velocity),
        n_gx, n_gy,
    )

    info, terms = pl.pallas_call(
        functools.partial(sample_kernel, rotors, cx_n, cy_n, tiles_z, full_y, points_n, n_gy),
        out_shape=(
            jax.ShapeDtypeStruct((64,), jnp.int32),
            jax.ShapeDtypeStruct((HOST_MAX, 16, LANES), f32),
        ),
        in_specs=[SMEM, HBM, HBM, HBM, HBM],
        out_specs=(SMEM, VMEM),
        scratch_shapes=[
            pltpu.SMEM((devices,), jnp.int32),
            pltpu.VMEM((HOST_MAX, 3, LANES), f32),
            pltpu.VMEM((HOST_MAX, 3, LANES), f32),
            pltpu.VMEM((HOST_MAX, 2, 3, BOX, cy_n, 128), f32),
            pltpu.VMEM((6 * BOX * BOX, 128), f32),
            pltpu.SemaphoreType.DMA((HOST_MAX, 4)),
        ],
        compiler_params=PARAMS,
        name="sample",
    )(meta, points, motion, velocity, cotangent)

    mid, *mid_faces, send, force = pl.pallas_call(
        functools.partial(advance_kernel, points_n, 2 * rotors, n_gx, n_gy),
        out_shape=(field, *faces, rows, jax.ShapeDtypeStruct((HOST_MAX, 8, LANES), f32)),
        in_specs=[SMEM, SMEM, VMEM, VMEM, HBM] + [VMEM] * 4,
        out_specs=(HBM,) + (VMEM,) * 6,
        scratch_shapes=[
            pltpu.VMEM(velocity.shape, f32),
            pltpu.VMEM(velocity.shape, f32),
            pltpu.VMEM((HOST_MAX, 3, BOX, cy_n, 128), f32),
            pltpu.VMEM((3 * BOX * BOX, 128), f32),
            pltpu.VMEM((3, BOX, cy_n, 128), f32),
            pltpu.SemaphoreType.DMA((6,)),
        ],
        compiler_params=PARAMS,
        name="advance",
    )(meta, info, terms, table, velocity, *halos)

    received = lax.all_to_all(send, AXES, 0, 0, tiled=True)
    halos = exchange(mid_faces, n_gx, n_gy)
    velocity_out = pl.pallas_call(
        functools.partial(finish_kernel, points_n, 2 * rotors, n_gx, n_gy),
        out_shape=field,
        in_specs=[SMEM, SMEM, VMEM, HBM] + [VMEM] * 4,
        out_specs=HBM,
        scratch_shapes=[
            pltpu.VMEM(velocity.shape, f32),
            pltpu.VMEM(velocity.shape, f32),
            pltpu.VMEM((HOST_MAX, 3, BOX, cy_n, 128), f32),
            pltpu.SemaphoreType.DMA((6,)),
        ],
        compiler_params=PARAMS,
        name="finish",
    )(meta, info, force, pltpu.with_memory_space_constraint(mid, pltpu.HBM), *halos)
    velocity_out, received = lax.optimization_barrier((velocity_out, received))
    return velocity_out, jnp.sum(received, axis=(0, 1))


def solution(mesh):
    cells = P(None, "gx", "gy", None)
    return jax.shard_map(
        per_device,
        mesh=mesh,
        in_specs=(cells, cells, P(), P(), P(AXES), P(), P()),
        out_specs=(cells, P(AXES)),
        check_vma=False,
    )
```

```python
import functools
import math

import jax
import jax.numpy as jnp
from jax import lax
from jax.experimental import pallas as pl
from jax.experimental.pallas import tpu as pltpu
from jax.sharding import PartitionSpec as P

AXES = ("gx", "gy")
HOST_MAX = 4
BOX = 4
LANES = 256
UNROLL = 14
FIELDS = 8

gauss_norm = math.pi ** (-1.5)
time_step = 0.5
viscosity = 0.15
HIGH = lax.Precision.HIGHEST

VMEM = pl.BlockSpec(memory_space=pltpu.VMEM)
SMEM = pl.BlockSpec(memory_space=pltpu.SMEM)
HBM = pl.BlockSpec(memory_space=pltpu.HBM)
PARAMS = pltpu.CompilerParams(vmem_limit_bytes=24 * 2**20)


def log2(value):
    bits = value.bit_length() - 1
    assert 1 << bits == value
    return bits


def gaussians(points, first_i, first_j, first_z, valid):
    cell_z = lax.broadcasted_iota(jnp.int32, (128, LANES), 0) + first_z
    delta_z = cell_z.astype(jnp.float32) - points[2:3]
    along_z = jnp.where(valid, gauss_norm * jnp.exp(-(delta_z * delta_z)), 0.0)
    tile = lax.broadcasted_iota(jnp.int32, (BOX * BOX, LANES), 0)
    delta_x = (lax.shift_right_logical(tile, 2) + first_i).astype(jnp.float32) - points[0:1]
    delta_y = ((tile & 3) + first_j).astype(jnp.float32) - points[1:2]
    across = jnp.exp(-(delta_x * delta_x + delta_y * delta_y))
    return along_z, across


def valid_lanes(odd, points_n):
    lane = lax.broadcasted_iota(jnp.int32, (1, LANES), 1)
    first = odd * (LANES - points_n)
    return (lane >= first) & (lane < first + points_n)


def rotor_at(info_ref, h):
    return [info_ref[h * FIELDS + f] for f in range(FIELDS)]


def reduce_tiles(product, across, k):
    rows = product[k * BOX * BOX : (k + 1) * BOX * BOX]
    return jnp.sum(rows * across, axis=0, keepdims=True)


def sample_kernel(
    rotors, cx_n, cy_n, tiles_z, full_y, points_n, n_gy,
    meta_ref, points_ref, motion_ref, velocity_ref, cotangent_ref,
    info_ref, terms_ref,
    seen_ref, point_ref, move_ref, block_ref, cell_ref, sems,
):
    log_t, log_y = log2(tiles_z), log2(full_y)
    log_cx, log_cy = log2(cx_n), log2(cy_n)
    gx, gy = meta_ref[2 * rotors], meta_ref[2 * rotors + 1]

    def clear(d, carry):
        seen_ref[d] = 0
        return carry

    lax.fori_loop(0, seen_ref.shape[0], clear, 0, unroll=16)

    def visit(r, count):
        tile = meta_ref[r]
        i = lax.shift_right_logical(tile, log_t + log_y)
        j = lax.shift_right_logical(tile, log_t) & (full_y - 1)
        mine = (lax.shift_right_logical(i, log_cx) == gx) & (lax.shift_right_logical(j, log_cy) == gy)
        own = meta_ref[rotors + r]
        earlier = seen_ref[own]
        seen_ref[own] = earlier + 1

        @pl.when(mine)
        def _():
            base = count * FIELDS
            info_ref[base] = r
            info_ref[base + 1] = i
            info_ref[base + 2] = j
            info_ref[base + 3] = tile & (tiles_z - 1)
            info_ref[base + 4] = own
            info_ref[base + 5] = earlier

        return count + mine.astype(jnp.int32)

    count = lax.fori_loop(0, rotors, visit, jnp.int32(0), unroll=8)
    info_ref[HOST_MAX * FIELDS] = count

    def copies(h):
        r, i, _, kz, _, _, _, _ = rotor_at(info_ref, h)
        start = lax.shift_right_logical(r, 1) * (2 * points_n) + (r & 1) * 128
        lanes = pl.ds(pl.multiple_of(start, 128), LANES)
        cells = pl.ds(pl.multiple_of(kz * 128, 128), 128)
        planes = pl.ds(i & (cx_n - 1), BOX)
        return [
            pltpu.make_async_copy(points_ref.at[:, lanes], point_ref.at[h], sems.at[h, 0]),
            pltpu.make_async_copy(motion_ref.at[:, lanes], move_ref.at[h], sems.at[h, 1]),
            pltpu.make_async_copy(velocity_ref.at[:, planes, :, cells], block_ref.at[h, 0], sems.at[h, 2]),
            pltpu.make_async_copy(cotangent_ref.at[:, planes, :, cells], block_ref.at[h, 1], sems.at[h, 3]),
        ]

    for h in range(HOST_MAX):

        @pl.when(h < count)
        def _(h=h):
            for copy in copies(h):
                copy.start()

    for h in range(HOST_MAX):

        @pl.when(h < count)
        def _(h=h):
            for copy in copies(h):
                copy.wait()
            r, i, j, kz, _, _, _, _ = rotor_at(info_ref, h)
            points, move = point_ref[h], move_ref[h]
            along_z, across = gaussians(points, i, j, kz * 128, valid_lanes(r & 1, points_n))
            rows = pl.ds(j & (cy_n - 1), BOX)
            for field in range(2):
                for k in range(3):
                    for a in range(BOX):
                        at = ((field * 3 + k) * BOX + a) * BOX
                        cell_ref[at : at + BOX, :] = block_ref[h, field, k, a, rows, :]
            product = jnp.dot(cell_ref[...], along_z, precision=HIGH, preferred_element_type=jnp.float32)
            relative = [reduce_tiles(product, across, k) - move[k : k + 1] for k in range(3)]
            speed = jnp.sqrt(sum(v * v for v in relative))
            for k in range(3):
                terms_ref[h, k : k + 1, :] = speed * relative[k]
                terms_ref[h, 3 + k : 4 + k, :] = reduce_tiles(product, across, 3 + k)
                terms_ref[h, 6 + k : 7 + k, :] = points[k : k + 1]
                terms_ref[h, 9 + k : 10 + k, :] = move[k : k + 1]


def spread(along_z, across, force, part_ref, h, j):
    weighted = jnp.concatenate([across * force[k] for k in range(3)], axis=0)
    contrib = lax.dot_general(
        weighted, along_z, (((1,), (1,)), ((), ())), precision=HIGH, preferred_element_type=jnp.float32
    )
    part_ref[h] = jnp.zeros(part_ref.shape[1:], jnp.float32)
    for k in range(3):
        for a in range(BOX):
            at = (k * BOX + a) * BOX
            part_ref[h, k, a, pl.ds(j, BOX)] = time_step * contrib[at : at + BOX]


def add_forces(info_ref, count, part_ref, next_ref, k):
    cx_n = next_ref.shape[1]
    for h in range(HOST_MAX):

        @pl.when(h < count)
        def _(h=h):
            _, i, _, kz, _, _, _, _ = rotor_at(info_ref, h)
            cells = pl.ds(pl.multiple_of(kz * 128, 128), 128)
            where = (k, pl.ds(i & (cx_n - 1), BOX), slice(None), cells)
            next_ref[where] = next_ref[where] + part_ref[h, k]


def laplace(meta_ref, gx_at, n_gx, n_gy, now_ref, halo_refs, next_ref, before, after_each):
    x_low_ref, x_high_ref, y_low_ref, y_high_ref = halo_refs
    _, cx_n, cy_n, cz_n = now_ref.shape
    gx, gy = meta_ref[gx_at], meta_ref[gx_at + 1]
    rate = time_step * viscosity
    subs, tiles = cy_n // 8, cz_n // 128
    row = lax.broadcasted_iota(jnp.int32, (8, 128), 0)
    lane = lax.broadcasted_iota(jnp.int32, (8, 128), 1)
    first_row, last_row, first_lane, last_lane = row == 0, row == 7, lane == 0, lane == 127
    zero = jnp.zeros((8, 128), jnp.float32)

    def flag(condition):
        return jnp.where(condition, 1.0, 0.0).astype(jnp.float32)

    has_x_low, has_x_high = flag(gx > 0), flag(gx < n_gx - 1)
    has_y_low, has_y_high = flag(gy > 0), flag(gy < n_gy - 1)

    def plane(k, x, below, above):
        def at(s, j):
            return now_ref[k, x, s * 8 : s * 8 + 8, j * 128 : j * 128 + 128]

        now = [[at(s, j) for j in range(tiles)] for s in range(subs)]
        for j in range(tiles):
            lanes = slice(j * 128, j * 128 + 128)
            up = [pltpu.roll(now[s][j], 1, 0) for s in range(subs)]
            down = [pltpu.roll(now[s][j], 7, 0) for s in range(subs)]
            low = jnp.broadcast_to(y_low_ref[k, x, :, lanes] * has_y_low, (8, 128))
            high = jnp.broadcast_to(y_high_ref[k, x, :, lanes] * has_y_high, (8, 128))
            for s in range(subs):
                here = now[s][j]
                y_below = jnp.where(first_row, up[s - 1] if s else low, up[s])
                y_above = jnp.where(last_row, down[s + 1] if s < subs - 1 else high, down[s])
                before = pltpu.roll(now[s][j - 1], 1, 1) if j else zero
                after = pltpu.roll(now[s][j + 1], 127, 1) if j < tiles - 1 else zero
                z_below = jnp.where(first_lane, before, pltpu.roll(here, 1, 1))
                z_above = jnp.where(last_lane, after, pltpu.roll(here, 127, 1))
                total = (below(s, j) + above(s, j)) + (y_below + y_above) + (z_below + z_above)
                next_ref[k, x, s * 8 : s * 8 + 8, lanes] = (1.0 - 6.0 * rate) * here + rate * total

    def inside(k, x):
        return lambda s, j: now_ref[k, x, s * 8 : s * 8 + 8, j * 128 : j * 128 + 128]

    def outside(ref, k, scale):
        return lambda s, j: ref[k, s * 8 : s * 8 + 8, j * 128 : j * 128 + 128] * scale

    def component(k, carry):
        before(k)
        plane(k, 0, outside(x_low_ref, k, has_x_low), inside(k, 1))
        plane(k, cx_n - 1, inside(k, cx_n - 2), outside(x_high_ref, k, has_x_high))

        def inner(x, carry):
            plane(k, x, inside(k, x - 1), inside(k, x + 1))
            return carry

        lax.fori_loop(1, cx_n - 1, inner, 0, unroll=UNROLL)
        after_each(k)
        return carry

    lax.fori_loop(0, 3, component, 0)


def aligned(value, rank, odd, points_n):
    earlier = pltpu.roll(value, LANES - points_n, 1)
    later = pltpu.roll(value, points_n, 1)
    return jnp.where(rank == odd, value, jnp.where(rank < odd, earlier, later))


def advance_kernel(
    points_n, gx_at, n_gx, n_gy,
    meta_ref, info_ref, terms_ref, table_ref, field_ref, hx_low_ref, hx_high_ref, hy_low_ref, hy_high_ref,
    out_ref, x_low_ref, x_high_ref, y_low_ref, y_high_ref, rows_ref, force_ref,
    now_ref, mid_ref, part_ref, cell_ref, block_ref, send_ref, sems,
):
    _, cx_n, cy_n, _ = now_ref.shape
    count = info_ref[HOST_MAX * FIELDS]

    def load(k):
        return pltpu.make_async_copy(field_ref.at[k], now_ref.at[k], sems.at[k])

    def save(k):
        return pltpu.make_async_copy(mid_ref.at[k], out_ref.at[k], sems.at[3 + k])

    for k in range(3):
        load(k).start()
    send_ref[...] = jnp.zeros_like(send_ref)

    def setup(h):
        r, i, j, kz, own, rank, _, _ = rotor_at(info_ref, h)
        along_z, across = gaussians(terms_ref[h, 6:9, :], i, j, kz * 128, valid_lanes(r & 1, points_n))
        row = table_ref[own]
        coef = jnp.where(rank > 0, row[:, 128:], row[:, :LANES])
        return along_z, across, (i & (cx_n - 1), j & (cy_n - 1), kz), aligned(coef, rank, r & 1, points_n)

    for h in range(HOST_MAX):

        @pl.when(h < count)
        def _(h=h):
            along_z, across, here, coef = setup(h)
            force = [coef * terms_ref[h, k : k + 1, :] for k in range(3)]
            spread(along_z, across, force, part_ref, h, here[1])

    def after(k):
        add_forces(info_ref, count, part_ref, mid_ref, k)
        save(k).start()

    halo_refs = (hx_low_ref, hx_high_ref, hy_low_ref, hy_high_ref)
    laplace(meta_ref, gx_at, n_gx, n_gy, now_ref, halo_refs, mid_ref, lambda k: load(k).wait(), after)

    for h in range(HOST_MAX):

        @pl.when(h < count)
        def _(h=h):
            along_z, across, (i, j, kz), coef = setup(h)
            r, _, _, _, own, rank, _, _ = rotor_at(info_ref, h)
            block_ref[...] = mid_ref[:, pl.ds(i, BOX), :, pl.ds(pl.multiple_of(kz * 128, 128), 128)]
            for k in range(3):
                for a in range(BOX):
                    at = (k * BOX + a) * BOX
                    cell_ref[at : at + BOX, :] = block_ref[k, a, pl.ds(j, BOX)]
            product = jnp.dot(cell_ref[...], along_z, precision=HIGH, preferred_element_type=jnp.float32)
            relative = [reduce_tiles(product, across, k) - terms_ref[h, 9 + k : 10 + k, :] for k in range(3)]
            speed = jnp.sqrt(sum(v * v for v in relative))
            grad = jnp.zeros((1, LANES), jnp.float32)
            for k in range(3):
                shape_term = speed * relative[k]
                grad = grad + terms_ref[h, 3 + k : 4 + k, :] * shape_term
                force_ref[h, k : k + 1, :] = coef * shape_term
            for k in range(3):
                force_ref[h, 3 + k : 4 + k, :] = terms_ref[h, 6 + k : 7 + k, :]
            grad = aligned(time_step * grad, r & 1, rank, points_n)
            blank = jnp.zeros((1, 128), jnp.float32)
            wide = jnp.where(
                rank > 0, jnp.concatenate([blank, grad], axis=1), jnp.concatenate([grad, blank], axis=1)
            )
            send_ref[own] = send_ref[own] + wide

    store = pltpu.make_async_copy(send_ref, rows_ref, sems.at[6])
    store.start()
    for k in range(3):
        write_faces(mid_ref, x_low_ref, x_high_ref, y_low_ref, y_high_ref, k)
    store.wait()
    for k in range(3):
        save(k).wait()


def write_faces(field_ref, x_low_ref, x_high_ref, y_low_ref, y_high_ref, k):
    _, cx_n, cy_n, _ = field_ref.shape
    x_low_ref[k] = field_ref[k, 0]
    x_high_ref[k] = field_ref[k, cx_n - 1]
    for x in range(cx_n):
        y_low_ref[k, x] = field_ref[k, x, 0:1]
        y_high_ref[k, x] = field_ref[k, x, cy_n - 1 : cy_n]


def faces_kernel(
    coef_ref, field_ref, out_ref, x_low_ref, x_high_ref, y_low_ref, y_high_ref, row_ref, table_ref, now_ref, sems
):
    def load(k):
        return pltpu.make_async_copy(field_ref.at[k], now_ref.at[k], sems.at[k])

    fetch = pltpu.make_async_copy(coef_ref, row_ref, sems.at[3])
    fetch.start()
    for k in range(3):
        load(k).start()
    fetch.wait()
    table_ref[...] = jnp.broadcast_to(row_ref[...].reshape(1, 1, row_ref.shape[0]), table_ref.shape)
    store = pltpu.make_async_copy(table_ref, out_ref, sems.at[4])
    store.start()
    for k in range(3):
        load(k).wait()
        write_faces(now_ref, x_low_ref, x_high_ref, y_low_ref, y_high_ref, k)
    store.wait()


def finish_kernel(
    points_n, gx_at, n_gx, n_gy,
    meta_ref, info_ref, force_ref, field_ref, x_low_ref, x_high_ref, y_low_ref, y_high_ref,
    out_ref,
    now_ref, next_ref, part_ref, sems,
):
    _, cx_n, cy_n, _ = now_ref.shape

    def load(k):
        return pltpu.make_async_copy(field_ref.at[k], now_ref.at[k], sems.at[k])

    def save(k):
        return pltpu.make_async_copy(next_ref.at[k], out_ref.at[k], sems.at[3 + k])

    for k in range(3):
        load(k).start()
    count = info_ref[HOST_MAX * FIELDS]
    for h in range(HOST_MAX):

        @pl.when(h < count)
        def _(h=h):
            r, i, j, kz, _, _, _, _ = rotor_at(info_ref, h)
            along_z, across = gaussians(force_ref[h, 3:6, :], i, j, kz * 128, valid_lanes(r & 1, points_n))
            force = [force_ref[h, k : k + 1, :] for k in range(3)]
            spread(along_z, across, force, part_ref, h, j & (cy_n - 1))

    def after(k):
        add_forces(info_ref, count, part_ref, next_ref, k)
        save(k).start()

    halo_refs = (x_low_ref, x_high_ref, y_low_ref, y_high_ref)
    laplace(meta_ref, gx_at, n_gx, n_gy, now_ref, halo_refs, next_ref, lambda k: load(k).wait(), after)
    for k in range(3):
        save(k).wait()


def ring(count, step):
    return [(i, (i + step) % count) for i in range(count)]


def exchange(faces, n_gx, n_gy):
    x_low, x_high, y_low, y_high = faces
    return (
        lax.ppermute(x_high, "gx", ring(n_gx, 1)),
        lax.ppermute(x_low, "gx", ring(n_gx, -1)),
        lax.ppermute(y_high, "gy", ring(n_gy, 1)),
        lax.ppermute(y_low, "gy", ring(n_gy, -1)),
    )


def per_device(velocity, cotangent, points, motion, coef, readers, owner):
    velocity, cotangent, points, motion = (
        pltpu.with_memory_space_constraint(array, pltpu.HBM) for array in (velocity, cotangent, points, motion)
    )
    _, cx_n, cy_n, cz_n = velocity.shape
    tiles_z = cz_n // 128
    n_gx, n_gy = lax.axis_size("gx"), lax.axis_size("gy")
    devices = n_gx * n_gy
    full_y = cy_n * n_gy
    rotors = readers.shape[0]
    points_n = points.shape[1] // rotors
    own_n = coef.shape[0]
    f32 = jnp.float32
    field = pltpu.HBM(velocity.shape, f32)
    face_x = jax.ShapeDtypeStruct((3, cy_n, cz_n), f32)
    face_y = jax.ShapeDtypeStruct((3, cx_n, 1, cz_n), f32)
    faces = (face_x, face_x, face_y, face_y)
    rows = pltpu.HBM((devices, 1, own_n), f32)

    meta = jnp.concatenate(
        [readers[:, 0], owner, lax.axis_index("gx")[None], lax.axis_index("gy")[None]]
    ).astype(jnp.int32)
    table, *first_faces = pl.pallas_call(
        faces_kernel,
        out_shape=(rows, *faces),
        in_specs=[HBM, HBM],
        out_specs=(HBM,) + (VMEM,) * 4,
        scratch_shapes=[
            pltpu.VMEM((own_n,), f32),
            pltpu.VMEM((devices, 1, own_n), f32),
            pltpu.VMEM(velocity.shape, f32),
            pltpu.SemaphoreType.DMA((5,)),
        ],
        compiler_params=PARAMS,
        name="faces",
    )(pltpu.with_memory_space_constraint(coef, pltpu.HBM), velocity)
    table = lax.all_to_all(table, AXES, 0, 0, tiled=True)
    halos = exchange(first_faces, n_gx, n_gy)

    info, terms = pl.pallas_call(
        functools.partial(sample_kernel, rotors, cx_n, cy_n, tiles_z, full_y, points_n, n_gy),
        out_shape=(
            jax.ShapeDtypeStruct((64,), jnp.int32),
            jax.ShapeDtypeStruct((HOST_MAX, 16, LANES), f32),
        ),
        in_specs=[SMEM, HBM, HBM, HBM, HBM],
        out_specs=(SMEM, VMEM),
        scratch_shapes=[
            pltpu.SMEM((devices,), jnp.int32),
            pltpu.VMEM((HOST_MAX, 3, LANES), f32),
            pltpu.VMEM((HOST_MAX, 3, LANES), f32),
            pltpu.VMEM((HOST_MAX, 2, 3, BOX, cy_n, 128), f32),
            pltpu.VMEM((6 * BOX * BOX, 128), f32),
            pltpu.SemaphoreType.DMA((HOST_MAX, 4)),
        ],
        compiler_params=PARAMS,
        cost_estimate=pl.CostEstimate(flops=2**33, transcendentals=0, bytes_accessed=2**26),
        name="sample",
    )(meta, points, motion, velocity, cotangent)

    mid, *mid_faces, send, force = pl.pallas_call(
        functools.partial(advance_kernel, points_n, 2 * rotors, n_gx, n_gy),
        out_shape=(field, *faces, rows, jax.ShapeDtypeStruct((HOST_MAX, 8, LANES), f32)),
        in_specs=[SMEM, SMEM, VMEM, VMEM, HBM] + [VMEM] * 4,
        out_specs=(HBM,) + (VMEM,) * 4 + (HBM, VMEM),
        scratch_shapes=[
            pltpu.VMEM(velocity.shape, f32),
            pltpu.VMEM(velocity.shape, f32),
            pltpu.VMEM((HOST_MAX, 3, BOX, cy_n, 128), f32),
            pltpu.VMEM((3 * BOX * BOX, 128), f32),
            pltpu.VMEM((3, BOX, cy_n, 128), f32),
            pltpu.VMEM((devices, 1, own_n), f32),
            pltpu.SemaphoreType.DMA((7,)),
        ],
        compiler_params=PARAMS,
        name="advance",
    )(meta, info, terms, table, velocity, *halos)

    received = lax.all_to_all(send, AXES, 0, 0, tiled=True)
    halos = exchange(mid_faces, n_gx, n_gy)
    velocity_out = pl.pallas_call(
        functools.partial(finish_kernel, points_n, 2 * rotors, n_gx, n_gy),
        out_shape=field,
        in_specs=[SMEM, SMEM, VMEM, HBM] + [VMEM] * 4,
        out_specs=HBM,
        scratch_shapes=[
            pltpu.VMEM(velocity.shape, f32),
            pltpu.VMEM(velocity.shape, f32),
            pltpu.VMEM((HOST_MAX, 3, BOX, cy_n, 128), f32),
            pltpu.SemaphoreType.DMA((6,)),
        ],
        compiler_params=PARAMS,
        name="finish",
    )(meta, info, force, pltpu.with_memory_space_constraint(mid, pltpu.HBM), *halos)
    velocity_out, received = lax.optimization_barrier((velocity_out, received))
    return velocity_out, jnp.sum(received, axis=(0, 1))


def solution(mesh):
    cells = P(None, "gx", "gy", None)
    return jax.shard_map(
        per_device,
        mesh=mesh,
        in_specs=(cells, cells, P(), P(), P(AXES), P(), P()),
        out_specs=(cells, P(AXES)),
        check_vma=False,
    )
```

```python
import functools
import math

import jax
import jax.numpy as jnp
from jax import lax
from jax.experimental import pallas as pl
from jax.experimental.pallas import tpu as pltpu
from jax.sharding import PartitionSpec as P

AXES = ("gx", "gy")
HOST_MAX = 4
BOX = 4
LANES = 256
UNROLL = 14
FIELDS = 8

gauss_norm = math.pi ** (-1.5)
time_step = 0.5
viscosity = 0.15
HIGH = lax.Precision.HIGHEST

VMEM = pl.BlockSpec(memory_space=pltpu.VMEM)
SMEM = pl.BlockSpec(memory_space=pltpu.SMEM)
HBM = pl.BlockSpec(memory_space=pltpu.HBM)
PARAMS = pltpu.CompilerParams(vmem_limit_bytes=24 * 2**20)


def log2(value):
    bits = value.bit_length() - 1
    assert 1 << bits == value
    return bits


def gaussians(points, first_i, first_j, first_z, valid):
    cell_z = lax.broadcasted_iota(jnp.int32, (128, LANES), 0) + first_z
    delta_z = cell_z.astype(jnp.float32) - points[2:3]
    along_z = jnp.where(valid, gauss_norm * jnp.exp(-(delta_z * delta_z)), 0.0)
    tile = lax.broadcasted_iota(jnp.int32, (BOX * BOX, LANES), 0)
    delta_x = (lax.shift_right_logical(tile, 2) + first_i).astype(jnp.float32) - points[0:1]
    delta_y = ((tile & 3) + first_j).astype(jnp.float32) - points[1:2]
    across = jnp.exp(-(delta_x * delta_x + delta_y * delta_y))
    return along_z, across


def valid_lanes(odd, points_n):
    lane = lax.broadcasted_iota(jnp.int32, (1, LANES), 1)
    first = odd * (LANES - points_n)
    return (lane >= first) & (lane < first + points_n)


def rotor_at(info_ref, h):
    return [info_ref[h * FIELDS + f] for f in range(FIELDS)]


def reduce_tiles(product, across, k):
    rows = product[k * BOX * BOX : (k + 1) * BOX * BOX]
    return jnp.sum(rows * across, axis=0, keepdims=True)


def search(rotors, cx_n, cy_n, tiles_z, full_y, at_ref, tiles_ref, owner_ref, owners_ref, info_ref, found_ref):
    log_t, log_y = log2(tiles_z), log2(full_y)
    log_cx, log_cy = log2(cx_n), log2(cy_n)
    gx, gy = at_ref[0], at_ref[1]
    for h in range(HOST_MAX + 1):
        found_ref[h] = 0

    def visit(r, count):
        tile = tiles_ref[0, r]
        x = lax.shift_right_logical(tile, log_t + log_y + log_cx)
        y = lax.shift_right_logical(tile, log_t + log_cy) & ((full_y >> log_cy) - 1)
        found_ref[count] = r
        return count + ((x == gx) & (y == gy)).astype(jnp.int32)

    count = lax.fori_loop(0, rotors, visit, jnp.int32(0), unroll=16)
    info_ref[HOST_MAX * FIELDS] = count
    owners = owners_ref[...]
    lane = lax.broadcasted_iota(jnp.int32, owners.shape, 1)
    chosen = [found_ref[h] for h in range(HOST_MAX)]
    earlier = [jnp.sum(jnp.where((owners == owner_ref[r]) & (lane < r), 1.0, 0.0)) for r in chosen]
    for h, r in enumerate(chosen):
        tile = tiles_ref[0, r]
        base = h * FIELDS
        info_ref[base] = r
        info_ref[base + 1] = lax.shift_right_logical(tile, log_t + log_y)
        info_ref[base + 2] = lax.shift_right_logical(tile, log_t) & (full_y - 1)
        info_ref[base + 3] = tile & (tiles_z - 1)
        info_ref[base + 4] = owner_ref[r]
        info_ref[base + 5] = earlier[h].astype(jnp.int32)
        info_ref[base + 6] = 0
        info_ref[base + 7] = 0


def sample_kernel(
    rotors, cx_n, cy_n, tiles_z, full_y, points_n,
    at_ref, owner_ref, owners_ref, tiles_ref, points_ref, motion_ref, velocity_ref, cotangent_ref,
    info_ref, terms_ref,
    found_ref, point_ref, move_ref, block_ref, cell_ref, sems,
):
    search(rotors, cx_n, cy_n, tiles_z, full_y, at_ref, tiles_ref, owner_ref, owners_ref, info_ref, found_ref)
    count = info_ref[HOST_MAX * FIELDS]

    def copies(h):
        r, i, _, kz, _, _, _, _ = rotor_at(info_ref, h)
        start = lax.shift_right_logical(r, 1) * (2 * points_n) + (r & 1) * 128
        lanes = pl.ds(pl.multiple_of(start, 128), LANES)
        cells = pl.ds(pl.multiple_of(kz * 128, 128), 128)
        planes = pl.ds(i & (cx_n - 1), BOX)
        return [
            pltpu.make_async_copy(points_ref.at[:, lanes], point_ref.at[h], sems.at[h, 0]),
            pltpu.make_async_copy(motion_ref.at[:, lanes], move_ref.at[h], sems.at[h, 1]),
            pltpu.make_async_copy(velocity_ref.at[:, planes, :, cells], block_ref.at[h, 0], sems.at[h, 2]),
            pltpu.make_async_copy(cotangent_ref.at[:, planes, :, cells], block_ref.at[h, 1], sems.at[h, 3]),
        ]

    for h in range(HOST_MAX):

        @pl.when(h < count)
        def _(h=h):
            for copy in copies(h):
                copy.start()

    for h in range(HOST_MAX):

        @pl.when(h < count)
        def _(h=h):
            for copy in copies(h):
                copy.wait()
            r, i, j, kz, _, _, _, _ = rotor_at(info_ref, h)
            points, move = point_ref[h], move_ref[h]
            along_z, across = gaussians(points, i, j, kz * 128, valid_lanes(r & 1, points_n))
            rows = pl.ds(j & (cy_n - 1), BOX)
            for field in range(2):
                for k in range(3):
                    for a in range(BOX):
                        at = ((field * 3 + k) * BOX + a) * BOX
                        cell_ref[at : at + BOX, :] = block_ref[h, field, k, a, rows, :]
            product = jnp.dot(cell_ref[...], along_z, precision=HIGH, preferred_element_type=jnp.float32)
            relative = [reduce_tiles(product, across, k) - move[k : k + 1] for k in range(3)]
            speed = jnp.sqrt(sum(v * v for v in relative))
            for k in range(3):
                terms_ref[h, k : k + 1, :] = speed * relative[k]
                terms_ref[h, 3 + k : 4 + k, :] = reduce_tiles(product, across, 3 + k)
                terms_ref[h, 6 + k : 7 + k, :] = points[k : k + 1]
                terms_ref[h, 9 + k : 10 + k, :] = move[k : k + 1]


def spread(along_z, across, force, part_ref, h, j):
    weighted = jnp.concatenate([across * force[k] for k in range(3)], axis=0)
    contrib = lax.dot_general(
        weighted, along_z, (((1,), (1,)), ((), ())), precision=HIGH, preferred_element_type=jnp.float32
    )
    part_ref[h] = jnp.zeros(part_ref.shape[1:], jnp.float32)
    for k in range(3):
        for a in range(BOX):
            at = (k * BOX + a) * BOX
            part_ref[h, k, a, pl.ds(j, BOX)] = time_step * contrib[at : at + BOX]


def add_forces(info_ref, count, part_ref, next_ref, k):
    cx_n = next_ref.shape[1]
    for h in range(HOST_MAX):

        @pl.when(h < count)
        def _(h=h):
            _, i, _, kz, _, _, _, _ = rotor_at(info_ref, h)
            cells = pl.ds(pl.multiple_of(kz * 128, 128), 128)
            where = (k, pl.ds(i & (cx_n - 1), BOX), slice(None), cells)
            next_ref[where] = next_ref[where] + part_ref[h, k]


def laplace(at_ref, n_gx, n_gy, now_ref, halo_refs, next_ref, before, after_each):
    x_low_ref, x_high_ref, y_low_ref, y_high_ref = halo_refs
    _, cx_n, cy_n, cz_n = now_ref.shape
    gx, gy = at_ref[0], at_ref[1]
    rate = time_step * viscosity
    subs, tiles = cy_n // 8, cz_n // 128
    row = lax.broadcasted_iota(jnp.int32, (8, 128), 0)
    lane = lax.broadcasted_iota(jnp.int32, (8, 128), 1)
    first_row, last_row, first_lane, last_lane = row == 0, row == 7, lane == 0, lane == 127
    zero = jnp.zeros((8, 128), jnp.float32)

    def flag(condition):
        return jnp.where(condition, 1.0, 0.0).astype(jnp.float32)

    has_x_low, has_x_high = flag(gx > 0), flag(gx < n_gx - 1)
    has_y_low, has_y_high = flag(gy > 0), flag(gy < n_gy - 1)

    def plane(k, x, below, above):
        def at(s, j):
            return now_ref[k, x, s * 8 : s * 8 + 8, j * 128 : j * 128 + 128]

        now = [[at(s, j) for j in range(tiles)] for s in range(subs)]
        for j in range(tiles):
            lanes = slice(j * 128, j * 128 + 128)
            up = [pltpu.roll(now[s][j], 1, 0) for s in range(subs)]
            down = [pltpu.roll(now[s][j], 7, 0) for s in range(subs)]
            low = jnp.broadcast_to(y_low_ref[k, x, :, lanes] * has_y_low, (8, 128))
            high = jnp.broadcast_to(y_high_ref[k, x, :, lanes] * has_y_high, (8, 128))
            for s in range(subs):
                here = now[s][j]
                y_below = jnp.where(first_row, up[s - 1] if s else low, up[s])
                y_above = jnp.where(last_row, down[s + 1] if s < subs - 1 else high, down[s])
                before = pltpu.roll(now[s][j - 1], 1, 1) if j else zero
                after = pltpu.roll(now[s][j + 1], 127, 1) if j < tiles - 1 else zero
                z_below = jnp.where(first_lane, before, pltpu.roll(here, 1, 1))
                z_above = jnp.where(last_lane, after, pltpu.roll(here, 127, 1))
                total = (below(s, j) + above(s, j)) + (y_below + y_above) + (z_below + z_above)
                next_ref[k, x, s * 8 : s * 8 + 8, lanes] = (1.0 - 6.0 * rate) * here + rate * total

    def inside(k, x):
        return lambda s, j: now_ref[k, x, s * 8 : s * 8 + 8, j * 128 : j * 128 + 128]

    def outside(ref, k, scale):
        return lambda s, j: ref[k, s * 8 : s * 8 + 8, j * 128 : j * 128 + 128] * scale

    def component(k, carry):
        before(k)
        plane(k, 0, outside(x_low_ref, k, has_x_low), inside(k, 1))
        plane(k, cx_n - 1, inside(k, cx_n - 2), outside(x_high_ref, k, has_x_high))

        def inner(x, carry):
            plane(k, x, inside(k, x - 1), inside(k, x + 1))
            return carry

        lax.fori_loop(1, cx_n - 1, inner, 0, unroll=UNROLL)
        after_each(k)
        return carry

    for k in range(3):
        component(k, 0)


def aligned(value, rank, odd, points_n):
    earlier = pltpu.roll(value, LANES - points_n, 1)
    later = pltpu.roll(value, points_n, 1)
    return jnp.where(rank == odd, value, jnp.where(rank < odd, earlier, later))


def advance_kernel(
    points_n, n_gx, n_gy,
    at_ref, info_ref, terms_ref, table_ref, field_ref, hx_low_ref, hx_high_ref, hy_low_ref, hy_high_ref,
    out_ref, x_low_ref, x_high_ref, y_low_ref, y_high_ref, rows_ref, force_ref,
    now_ref, mid_ref, part_ref, cell_ref, block_ref, send_ref, sems,
):
    _, cx_n, cy_n, _ = now_ref.shape
    count = info_ref[HOST_MAX * FIELDS]

    def load(k):
        return pltpu.make_async_copy(field_ref.at[k], now_ref.at[k], sems.at[k])

    def save(k):
        return pltpu.make_async_copy(mid_ref.at[k], out_ref.at[k], sems.at[3 + k])

    for k in range(3):
        load(k).start()
    send_ref[...] = jnp.zeros_like(send_ref)

    def setup(h):
        r, i, j, kz, own, rank, _, _ = rotor_at(info_ref, h)
        along_z, across = gaussians(terms_ref[h, 6:9, :], i, j, kz * 128, valid_lanes(r & 1, points_n))
        row = table_ref[own]
        coef = jnp.where(rank > 0, row[:, 128:], row[:, :LANES])
        return along_z, across, (i & (cx_n - 1), j & (cy_n - 1), kz), aligned(coef, rank, r & 1, points_n)

    for h in range(HOST_MAX):

        @pl.when(h < count)
        def _(h=h):
            along_z, across, here, coef = setup(h)
            force = [coef * terms_ref[h, k : k + 1, :] for k in range(3)]
            spread(along_z, across, force, part_ref, h, here[1])

    def after(k):
        add_forces(info_ref, count, part_ref, mid_ref, k)
        save(k).start()

    halo_refs = (hx_low_ref, hx_high_ref, hy_low_ref, hy_high_ref)
    laplace(at_ref, n_gx, n_gy, now_ref, halo_refs, mid_ref, lambda k: load(k).wait(), after)

    for h in range(HOST_MAX):

        @pl.when(h < count)
        def _(h=h):
            along_z, across, (i, j, kz), coef = setup(h)
            r, _, _, _, own, rank, _, _ = rotor_at(info_ref, h)
            block_ref[...] = mid_ref[:, pl.ds(i, BOX), :, pl.ds(pl.multiple_of(kz * 128, 128), 128)]
            for k in range(3):
                for a in range(BOX):
                    at = (k * BOX + a) * BOX
                    cell_ref[at : at + BOX, :] = block_ref[k, a, pl.ds(j, BOX)]
            product = jnp.dot(cell_ref[...], along_z, precision=HIGH, preferred_element_type=jnp.float32)
            relative = [reduce_tiles(product, across, k) - terms_ref[h, 9 + k : 10 + k, :] for k in range(3)]
            speed = jnp.sqrt(sum(v * v for v in relative))
            grad = jnp.zeros((1, LANES), jnp.float32)
            for k in range(3):
                shape_term = speed * relative[k]
                grad = grad + terms_ref[h, 3 + k : 4 + k, :] * shape_term
                force_ref[h, k : k + 1, :] = coef * shape_term
            for k in range(3):
                force_ref[h, 3 + k : 4 + k, :] = terms_ref[h, 6 + k : 7 + k, :]
            grad = aligned(time_step * grad, r & 1, rank, points_n)
            blank = jnp.zeros((1, 128), jnp.float32)
            wide = jnp.where(
                rank > 0, jnp.concatenate([blank, grad], axis=1), jnp.concatenate([grad, blank], axis=1)
            )
            send_ref[own] = send_ref[own] + wide

    store = pltpu.make_async_copy(send_ref, rows_ref, sems.at[6])
    store.start()
    for k in range(3):
        write_faces(mid_ref, x_low_ref, x_high_ref, y_low_ref, y_high_ref, k)
    store.wait()
    for k in range(3):
        save(k).wait()


def write_faces(field_ref, x_low_ref, x_high_ref, y_low_ref, y_high_ref, k):
    _, cx_n, cy_n, _ = field_ref.shape
    x_low_ref[k] = field_ref[k, 0]
    x_high_ref[k] = field_ref[k, cx_n - 1]
    for x in range(cx_n):
        y_low_ref[k, x] = field_ref[k, x, 0:1]
        y_high_ref[k, x] = field_ref[k, x, cy_n - 1 : cy_n]


def faces_kernel(
    coef_ref, field_ref, out_ref, x_low_ref, x_high_ref, y_low_ref, y_high_ref, row_ref, table_ref, now_ref, sems
):
    def load(k):
        return pltpu.make_async_copy(field_ref.at[k], now_ref.at[k], sems.at[k])

    fetch = pltpu.make_async_copy(coef_ref, row_ref, sems.at[3])
    fetch.start()
    for k in range(3):
        load(k).start()
    fetch.wait()
    table_ref[...] = jnp.broadcast_to(row_ref[...].reshape(1, 1, row_ref.shape[0]), table_ref.shape)
    store = pltpu.make_async_copy(table_ref, out_ref, sems.at[4])
    store.start()
    for k in range(3):
        load(k).wait()
        write_faces(now_ref, x_low_ref, x_high_ref, y_low_ref, y_high_ref, k)
    store.wait()


def finish_kernel(
    points_n, n_gx, n_gy,
    at_ref, info_ref, force_ref, field_ref, x_low_ref, x_high_ref, y_low_ref, y_high_ref,
    out_ref,
    now_ref, next_ref, part_ref, sems,
):
    _, cx_n, cy_n, _ = now_ref.shape

    def load(k):
        return pltpu.make_async_copy(field_ref.at[k], now_ref.at[k], sems.at[k])

    def save(k):
        return pltpu.make_async_copy(next_ref.at[k], out_ref.at[k], sems.at[3 + k])

    for k in range(3):
        load(k).start()
    count = info_ref[HOST_MAX * FIELDS]
    for h in range(HOST_MAX):

        @pl.when(h < count)
        def _(h=h):
            r, i, j, kz, _, _, _, _ = rotor_at(info_ref, h)
            along_z, across = gaussians(force_ref[h, 3:6, :], i, j, kz * 128, valid_lanes(r & 1, points_n))
            force = [force_ref[h, k : k + 1, :] for k in range(3)]
            spread(along_z, across, force, part_ref, h, j & (cy_n - 1))

    def after(k):
        add_forces(info_ref, count, part_ref, next_ref, k)
        save(k).start()

    halo_refs = (x_low_ref, x_high_ref, y_low_ref, y_high_ref)
    laplace(at_ref, n_gx, n_gy, now_ref, halo_refs, next_ref, lambda k: load(k).wait(), after)
    for k in range(3):
        save(k).wait()


def ring(count, step):
    return [(i, (i + step) % count) for i in range(count)]


def exchange(faces, n_gx, n_gy):
    x_low, x_high, y_low, y_high = faces
    return (
        lax.ppermute(x_high, "gx", ring(n_gx, 1)),
        lax.ppermute(x_low, "gx", ring(n_gx, -1)),
        lax.ppermute(y_high, "gy", ring(n_gy, 1)),
        lax.ppermute(y_low, "gy", ring(n_gy, -1)),
    )


def per_device(velocity, cotangent, points, motion, coef, readers, owner):
    velocity, cotangent, points, motion = (
        pltpu.with_memory_space_constraint(array, pltpu.HBM) for array in (velocity, cotangent, points, motion)
    )
    _, cx_n, cy_n, cz_n = velocity.shape
    tiles_z = cz_n // 128
    n_gx, n_gy = lax.axis_size("gx"), lax.axis_size("gy")
    devices = n_gx * n_gy
    full_y = cy_n * n_gy
    rotors = readers.shape[0]
    points_n = points.shape[1] // rotors
    own_n = coef.shape[0]
    f32 = jnp.float32
    field = pltpu.HBM(velocity.shape, f32)
    face_x = jax.ShapeDtypeStruct((3, cy_n, cz_n), f32)
    face_y = jax.ShapeDtypeStruct((3, cx_n, 1, cz_n), f32)
    faces = (face_x, face_x, face_y, face_y)
    rows = pltpu.HBM((devices, 1, own_n), f32)

    at = jnp.stack([lax.axis_index("gx"), lax.axis_index("gy")]).astype(jnp.int32)
    table, *first_faces = pl.pallas_call(
        faces_kernel,
        out_shape=(rows, *faces),
        in_specs=[HBM, HBM],
        out_specs=(HBM,) + (VMEM,) * 4,
        scratch_shapes=[
            pltpu.VMEM((own_n,), f32),
            pltpu.VMEM((devices, 1, own_n), f32),
            pltpu.VMEM(velocity.shape, f32),
            pltpu.SemaphoreType.DMA((5,)),
        ],
        compiler_params=PARAMS,
        name="faces",
    )(pltpu.with_memory_space_constraint(coef, pltpu.HBM), velocity)
    table = lax.all_to_all(table, AXES, 0, 0, tiled=True)
    halos = exchange(first_faces, n_gx, n_gy)

    info, terms = pl.pallas_call(
        functools.partial(sample_kernel, rotors, cx_n, cy_n, tiles_z, full_y, points_n),
        out_shape=(
            jax.ShapeDtypeStruct((64,), jnp.int32),
            jax.ShapeDtypeStruct((HOST_MAX, 16, LANES), f32),
        ),
        in_specs=[SMEM, SMEM, VMEM, SMEM] + [HBM] * 4,
        out_specs=(SMEM, VMEM),
        scratch_shapes=[
            pltpu.SMEM((HOST_MAX + 1,), jnp.int32),
            pltpu.VMEM((HOST_MAX, 3, LANES), f32),
            pltpu.VMEM((HOST_MAX, 3, LANES), f32),
            pltpu.VMEM((HOST_MAX, 2, 3, BOX, cy_n, 128), f32),
            pltpu.VMEM((6 * BOX * BOX, 128), f32),
            pltpu.SemaphoreType.DMA((HOST_MAX, 4)),
        ],
        compiler_params=PARAMS,
        cost_estimate=pl.CostEstimate(flops=2**33, transcendentals=0, bytes_accessed=2**26),
        name="sample",
    )(at, owner, owner.reshape(1, rotors), readers.T, points, motion, velocity, cotangent)

    mid, *mid_faces, send, force = pl.pallas_call(
        functools.partial(advance_kernel, points_n, n_gx, n_gy),
        out_shape=(field, *faces, rows, jax.ShapeDtypeStruct((HOST_MAX, 8, LANES), f32)),
        in_specs=[SMEM, SMEM, VMEM, VMEM, HBM] + [VMEM] * 4,
        out_specs=(HBM,) + (VMEM,) * 4 + (HBM, VMEM),
        scratch_shapes=[
            pltpu.VMEM(velocity.shape, f32),
            pltpu.VMEM(velocity.shape, f32),
            pltpu.VMEM((HOST_MAX, 3, BOX, cy_n, 128), f32),
            pltpu.VMEM((3 * BOX * BOX, 128), f32),
            pltpu.VMEM((3, BOX, cy_n, 128), f32),
            pltpu.VMEM((devices, 1, own_n), f32),
            pltpu.SemaphoreType.DMA((7,)),
        ],
        compiler_params=PARAMS,
        name="advance",
    )(at, info, terms, table, velocity, *halos)

    received = lax.all_to_all(send, AXES, 0, 0, tiled=True)
    halos = exchange(mid_faces, n_gx, n_gy)
    velocity_out = pl.pallas_call(
        functools.partial(finish_kernel, points_n, n_gx, n_gy),
        out_shape=field,
        in_specs=[SMEM, SMEM, VMEM, HBM] + [VMEM] * 4,
        out_specs=HBM,
        scratch_shapes=[
            pltpu.VMEM(velocity.shape, f32),
            pltpu.VMEM(velocity.shape, f32),
            pltpu.VMEM((HOST_MAX, 3, BOX, cy_n, 128), f32),
            pltpu.SemaphoreType.DMA((6,)),
        ],
        compiler_params=PARAMS,
        name="finish",
    )(at, info, force, pltpu.with_memory_space_constraint(mid, pltpu.HBM), *halos)
    velocity_out, received = lax.optimization_barrier((velocity_out, received))
    return velocity_out, jnp.sum(received, axis=(0, 1))


def solution(mesh):
    cells = P(None, "gx", "gy", None)
    return jax.shard_map(
        per_device,
        mesh=mesh,
        in_specs=(cells, cells, P(), P(), P(AXES), P(), P()),
        out_specs=(cells, P(AXES)),
        check_vma=False,
    )
```
